32 devices in a mesh: groups: 2 (over y), batch: 8 (over z, x), mp: 2 (over core).
Axes of the slice: x: 2, y: 2, z: 4, core: 2. Of those that a mesh axis runs over, the one named last changes fastest.
Arguments:
- tokens: bfloat16 [1024, 16384], P(('groups', 'batch')), parts along dimension 0, may hold values from -6 to 6
- gate_weight: bfloat16 [16384, 256], P('batch', 'mp'), may hold values from -0.046875 to 0.046875
- up_weight: bfloat16 [16384, 256], P('batch', 'mp'), may hold values from -0.046875 to 0.046875
- down_weight: bfloat16 [256, 16384], P('mp', 'batch'), may hold values from -0.5 to 0.5
Outputs:
- mixed: bfloat16 [1024, 16384], P(('groups', 'batch'), 'mp'), parts along dimension 0
The draws below stay inside these ranges and needn't reach their ends.
There are 2 independent parts, one for each index of `groups`. The reference program is written for one: setup_inputs(seed, part) draws one part's arguments, and reference() takes and returns one part's arrays. A program takes and returns all parts, laid end to end along the dimension named above; an argument that names none is the same for every part. Nothing has to cross between parts.
All inputs are finite; a program needn't handle non-finite values.
Results may differ from the reference program's by a relative error of at most 0.018.
Values may be sent and summed in bfloat16 or wider, within the bound.
No kernel may reach another device: no remote copies, remote signals or barrier semaphores. Data moves between devices by JAX's collectives and lax.ppermute only.
A program may use at most 64 MiB of HBM per device.

```python
import jax
import jax.numpy as jnp
from jax import lax

D = 16384
HID_DEV = 128
TOKENS = 512
FF = 256
N_MP = 2


def strengthened(drawn, stream_key, source, target, shards_of, factor):
    def block_of(dim):
        return (jnp.arange(drawn.shape[dim]) // (drawn.shape[dim] // shards_of)).reshape((-1,) + (1,) * (drawn.ndim - 1 - dim))

    first = jax.random.permutation(stream_key, shards_of)[block_of(target)]
    other_side = (block_of(target) + shards_of // 2) % shards_of
    return jnp.where((block_of(source) == first) | (block_of(source) == other_side), factor * drawn, drawn)


def steps_of(stream_key, extent, shards, least, top_value):
    level, own = 1.0, jax.random.fold_in(stream_key, 6)
    for position, parts in shards:
        steps = jnp.exp(jax.random.uniform(jax.random.fold_in(own, position), (parts,), jnp.float32, least / len(shards), top_value / len(shards)))
        level = level * jnp.repeat(steps, extent[position] // parts).reshape([-1 if axis == position else 1 for axis in range(len(extent))])
    return level


def bell_draw(own_key, dims, spread, limit, split=(), held_as=jnp.bfloat16):
    drawn = spread * jax.random.normal(own_key, dims, jnp.float32)
    if split:
        drawn = drawn * steps_of(own_key, dims, split, -0.22, 0.18)
    return jnp.clip(drawn, -limit, limit).astype(held_as)


def bell_draw_with(own_key, extent, width, most, split, heavy, dtype=jnp.bfloat16):
    entries = width * jax.random.normal(own_key, extent, jnp.float32)
    if split:
        entries = entries * steps_of(own_key, extent, split, -0.22, 0.18)
    return jnp.clip(strengthened(entries, jax.random.fold_in(own_key, 3), *heavy), -most, most).astype(dtype)


def setup_inputs(seed: int = 0, part: int = 0) -> dict:
    key_list = jax.random.split(jax.random.key(seed), 5)
    part_keys = jax.random.split(jax.random.fold_in(key_list[4], part), 5)
    tokens = bell_draw(part_keys[0], (TOKENS, D), 1.0, 6.0, ((0, 8),))
    gate_weight = bell_draw(key_list[1], (D, FF), D ** -0.5, 0.046875, ((0, 8), (1, 2)))
    up_weight = bell_draw(key_list[2], (D, FF), D ** -0.5, 0.046875, ((0, 8), (1, 2)))
    down_weight = bell_draw_with(key_list[3], (FF, D), FF ** -0.5, 0.5, ((0, 2), (1, 8)), (0, 1, 8, 2.0))
    return dict(tokens=tokens, gate_weight=gate_weight, up_weight=up_weight, down_weight=down_weight)


def reference(tokens, gate_weight, up_weight, down_weight):
    gate = jnp.dot(tokens, gate_weight, preferred_element_type=jnp.float32)
    up = jnp.dot(tokens, up_weight, preferred_element_type=jnp.float32)
    hidden = (jax.nn.silu(gate) * up).astype(jnp.bfloat16)
    rows = hidden.shape[0]
    hidden_groups = jnp.transpose(hidden.reshape(rows, N_MP, HID_DEV), (1, 0, 2))
    down_groups = down_weight.reshape(N_MP, HID_DEV, down_weight.shape[1])

    def add_group(total, pair):
        partial_value = jnp.dot(pair[0], pair[1], preferred_element_type=jnp.float32).astype(jnp.bfloat16)
        partial_value = lax.optimization_barrier(partial_value)
        return total + partial_value.astype(jnp.float32), None

    start = jnp.zeros((rows, down_weight.shape[1]), jnp.float32)
    total, unused = lax.scan(add_group, start, (hidden_groups, down_groups))
    return total.astype(jnp.bfloat16)
```

```python
import functools

import jax
import jax.numpy as jnp
from jax import lax
from jax.sharding import PartitionSpec as P


def in_core_order(parts, core):
    if len(parts) == 2:
        first, second = parts
        return [jnp.where(core == 0, first, second), jnp.where(core == 0, second, first)]
    stack = jnp.take(jnp.stack(parts), core ^ jnp.arange(len(parts)), axis=0)
    return [stack[k] for k in range(len(parts))]


def per_device(tokens, gate_weight, up_weight, down_weight, *, n_batch, n_mp):
    n_row = n_batch // n_mp
    rows = tokens.shape[0]
    block, units = gate_weight.shape
    columns = down_weight.shape[1]
    axes = ("batch", "mp")
    batch = lax.axis_index("batch")
    core = lax.axis_index("mp")
    row = batch // n_mp

    def swap(value, step):
        pairs = [
            ((r * n_mp + lane) * n_mp + c, ((r ^ step) * n_mp + c) * n_mp + lane)
            for r in range(n_row)
            for lane in range(n_mp)
            for c in range(n_mp)
        ]
        return lax.ppermute(value, axes, pairs)

    def give_out(value, step):
        pairs = [
            (b * n_mp + c, ((((b % n_row) ^ step) * n_mp + c) * n_mp + b // n_row))
            for b in range(n_batch)
            for c in range(n_mp)
        ]
        return lax.ppermute(value, axes, pairs)

    def others(value):
        return [
            lax.ppermute(value, "mp", [(c, c ^ step) for c in range(n_mp)])
            for step in range(1, n_mp)
        ]

    order = list(range(n_row))[::-1]

    arrived = {}
    for step in order:
        start = ((row ^ step) * n_mp + core) * block
        arrived[step] = swap(lax.dynamic_slice_in_dim(tokens, start, block, 1), step)

    weight = jnp.concatenate([gate_weight, up_weight], axis=1)
    weights = jnp.concatenate(in_core_order([weight] + others(weight), core), axis=1)
    down = jnp.concatenate(in_core_order([down_weight] + others(down_weight), core), axis=0)

    total = None
    for step in order[::-1]:
        partial = jnp.dot(arrived[step], weights, preferred_element_type=jnp.float32)
        back = swap(partial.astype(jnp.bfloat16), step).astype(jnp.float32)
        total = back if total is None else total + back
    for part in others(total):
        total = total + part

    pairs = total.reshape(rows, n_mp, 2, units)
    hidden = (jax.nn.silu(pairs[:, :, 0]) * pairs[:, :, 1]).astype(jnp.bfloat16)
    hidden = hidden.reshape(rows, n_mp * units)

    their_hidden = {step: swap(hidden, step) for step in order}
    mixed = jnp.zeros((rows, n_row * columns), jnp.bfloat16)
    all_hidden = jnp.stack([their_hidden[step] for step in range(n_row)])
    for step in order:
        wanted = row ^ ((batch % n_row) ^ step)
        rows_of = lax.dynamic_index_in_dim(all_hidden, wanted, 0, keepdims=False)
        result = jnp.dot(rows_of, down, preferred_element_type=jnp.float32).astype(jnp.bfloat16)
        got = give_out(result, step)
        mixed = lax.dynamic_update_slice_in_dim(mixed, got, (row ^ step) * columns, 1)
    return mixed


def solution(mesh):
    return jax.shard_map(
        functools.partial(per_device, n_batch=mesh.shape["batch"], n_mp=mesh.shape["mp"]),
        mesh=mesh,
        in_specs=(
            P(("groups", "batch"), None),
            P("batch", "mp"),
            P("batch", "mp"),
            P("mp", "batch"),
        ),
        out_specs=P(("groups", "batch"), "mp"),
        check_vma=False,
    )
```

```python
import jax
import jax.numpy as jnp
from jax import lax
from jax.sharding import PartitionSpec as P


def in_order(parts, index):
    if len(parts) == 1:
        return parts
    if len(parts) == 2:
        first, second = parts
        return [jnp.where(index == 0, first, second), jnp.where(index == 0, second, first)]
    stack = jnp.take(jnp.stack(parts), index ^ jnp.arange(len(parts)), axis=0)
    return [stack[k] for k in range(len(parts))]


def per_device(tokens, gate_weight, up_weight, down_weight, *, n_groups, n_batch, n_mp):
    n_row = n_batch // n_mp
    rows = tokens.shape[0]
    block, units = gate_weight.shape
    columns = down_weight.shape[1]
    axes = ("batch", "mp")
    batch = lax.axis_index("batch")
    core = lax.axis_index("mp")
    group = lax.axis_index("groups")
    row = batch // n_mp
    lane = batch % n_mp
    halved = n_groups == 2 and n_mp == 2 and n_row % 2 == 0
    near = n_row // 2 if halved else n_row

    def device(r, a, c):
        return (r * n_mp + a) * n_mp + c

    every = [(r, a, c) for r in range(n_row) for a in range(n_mp) for c in range(n_mp)]

    def swap(value, step):
        return lax.ppermute(
            value, axes, [(device(r, a, c), device(r ^ step, c, a)) for r, a, c in every]
        )

    def give_out(value, step, turn):
        if halved:
            pairs = [(device(r, a, c), device(r ^ step, c, a ^ turn)) for r, a, c in every]
        else:
            pairs = [
                (device(r, a, c), device(((r * n_mp + a) % n_row) ^ step, c, (r * n_mp + a) // n_row))
                for r, a, c in every
            ]
        return lax.ppermute(value, axes, pairs)

    def others(value, axis, size):
        return [
            lax.ppermute(value, axis, [(c, c ^ step) for c in range(size)])
            for step in range(1, size)
        ]

    def cores(value):
        return in_order([value] + others(value, "mp", n_mp), core)

    order = list(range(n_row))[::-1]

    arrived = {}
    for step in order:
        start = ((row ^ step) * n_mp + core) * block
        sent = lax.dynamic_slice_in_dim(tokens, start, block, 1)
        arrived[step] = swap(sent, step)

    weights = cores(gate_weight) + cores(up_weight)
    weights = jnp.concatenate(weights, axis=1)
    downs = [jnp.concatenate(cores(down_weight), axis=0)]
    if halved:
        part = units // 2
        far = lax.dynamic_slice_in_dim(down_weight, group * part, part, 0)
        far = lax.ppermute(far, "batch", [(b, b ^ (near * n_mp)) for b in range(n_batch)])
        fars = in_order([far] + others(far, "groups", 2), group)
        far = jnp.concatenate(fars, axis=0)
        downs.append(jnp.concatenate(cores(far), axis=0))

    total = None
    for step in order[::-1]:
        partial = jnp.dot(arrived[step], weights, preferred_element_type=jnp.float32)
        back = swap(partial.astype(jnp.bfloat16), step)
        back = back.astype(jnp.float32)
        total = back if total is None else total + back
    for part in others(total, "mp", n_mp):
        total = total + part

    gate = total[:, : n_mp * units]
    up = total[:, n_mp * units :]
    hidden = (jax.nn.silu(gate) * up).astype(jnp.bfloat16)

    theirs = []
    for step in range(near):
        theirs.append(swap(hidden, step))
    mixed = jnp.zeros((rows, n_row * columns), jnp.bfloat16)
    if halved:
        stacked = jnp.concatenate(theirs, axis=0)
        both = [
            jnp.dot(stacked, down, preferred_element_type=jnp.float32).astype(jnp.bfloat16)
            for down in downs
        ]
        side = row // near
        for step in range(near)[::-1]:
            for turn in range(2):
                mine, other = (r[step * rows : (step + 1) * rows] for r in both)
                sent = jnp.where(lane ^ turn == side, mine, other)
                got = give_out(sent, step, turn)
                at = ((row % near) ^ step) * n_mp + (core ^ turn)
                mixed = lax.dynamic_update_slice_in_dim(mixed, got, at * columns, 1)
        return mixed
    stacked = jnp.stack(theirs)
    for step in order:
        wanted = row ^ (batch % n_row) ^ step
        hidden_rows = lax.dynamic_index_in_dim(stacked, wanted, 0, keepdims=False)
        result = jnp.dot(hidden_rows, downs[0], preferred_element_type=jnp.float32)
        got = give_out(result.astype(jnp.bfloat16), step, 0)
        mixed = lax.dynamic_update_slice_in_dim(mixed, got, (row ^ step) * columns, 1)
    return mixed


def solution(mesh):
    sizes = {f"n_{axis}": mesh.shape[axis] for axis in ("groups", "batch", "mp")}

    def body(*args):
        return per_device(*args, **sizes)

    return jax.shard_map(
        body,
        mesh=mesh,
        in_specs=(
            P(("groups", "batch"), None),
            P("batch", "mp"),
            P("batch", "mp"),
            P("mp", "batch"),
        ),
        out_specs=P(("groups", "batch"), "mp"),
        check_vma=False,
    )
```

```python
import functools

import jax
import jax.numpy as jnp
from jax import lax
from jax.experimental import pallas as pl
from jax.experimental.pallas import tpu as pltpu
from jax.sharding import PartitionSpec as P


def in_order(parts, index):
    if len(parts) == 1:
        return parts
    if len(parts) == 2:
        first, second = parts
        return [jnp.where(index == 0, first, second), jnp.where(index == 0, second, first)]
    stack = jnp.take(jnp.stack(parts), index ^ jnp.arange(len(parts)), axis=0)
    return [stack[k] for k in range(len(parts))]


def cut_kernel(place, tokens, *refs, size):
    slabs, sem = refs[:-1], refs[-1]
    block = slabs[0].shape[1] // 2
    first_row = pl.multiple_of(place[0], size)
    copies = []
    for k in range(2 * len(slabs)):
        column = pl.multiple_of(place[1 + k], block)
        copies.append(
            pltpu.make_async_copy(
                tokens.at[pl.ds(first_row, size), pl.ds(column, block)],
                slabs[k // 2].at[:, pl.ds(k % 2 * block, block)],
                sem.at[k],
            )
        )
    for copy in copies:
        copy.start()
    for copy in copies:
        copy.wait()


def cut(place, tokens, n_slab, size, depth):
    slab = jax.ShapeDtypeStruct((size, depth), tokens.dtype)
    return pl.pallas_call(
        functools.partial(cut_kernel, size=size),
        out_shape=[slab] * n_slab,
        in_specs=[pl.BlockSpec(memory_space=pltpu.SMEM), pl.BlockSpec(memory_space=pltpu.HBM)],
        out_specs=[pl.BlockSpec(memory_space=pltpu.VMEM)] * n_slab,
        scratch_shapes=[pltpu.SemaphoreType.DMA((2 * n_slab,))],
        compiler_params=pltpu.CompilerParams(vmem_limit_bytes=8 * 1024 * 1024),
        name="cut",
    )(place, tokens)


def sums_kernel(*refs, n_slab, n_part):
    slabs, weights = refs[:n_slab], refs[n_slab : n_slab + 2 * n_part * n_part]
    outs = refs[n_slab + len(weights) : -1]
    slab_buf = refs[-1]
    size = slabs[0].shape[0]
    block, units = weights[0].shape
    for k, slab in enumerate(slabs):
        slab_buf[k * size : (k + 1) * size] = slab[...]
    wide = n_part * units
    for kind in range(2):
        total = None
        for part in range(n_part):
            first = (part * 2 + kind) * n_part
            product = jnp.dot(
                slab_buf[:, part * block : (part + 1) * block],
                jnp.concatenate([w[...] for w in weights[first : first + n_part]], axis=1),
                preferred_element_type=jnp.float32,
            )
            total = product if total is None else total + product
        for k, out in enumerate(outs):
            part_of = total[k * size : (k + 1) * size]
            out[:, kind * wide : (kind + 1) * wide] = part_of.astype(out.dtype)


def slab_sums(slabs, weights, n_part):
    n_slab = len(slabs)
    size, depth = slabs[0].shape
    wide = 2 * n_part * weights[0].shape[1]
    kept = jax.ShapeDtypeStruct((size, wide), jnp.float32)
    sent = jax.ShapeDtypeStruct((size, wide), jnp.bfloat16)
    vmem = pl.BlockSpec(memory_space=pltpu.VMEM)
    return pl.pallas_call(
        functools.partial(sums_kernel, n_slab=n_slab, n_part=n_part),
        out_shape=[kept] + [sent] * (n_slab - 1),
        in_specs=[vmem] * (n_slab + len(weights)),
        out_specs=[vmem] * n_slab,
        scratch_shapes=[pltpu.VMEM((n_slab * size, depth), jnp.bfloat16)],
        compiler_params=pltpu.CompilerParams(vmem_limit_bytes=16 * 1024 * 1024),
        name="slab_sums",
    )(*slabs, *weights)


def place_kernel(index, *refs):
    blocks, (out, sem) = refs[:-2], refs[-2:]
    columns = blocks[0].shape[1]
    copies = []
    for k, block in enumerate(blocks):
        to = out.at[:, pl.ds(pl.multiple_of((index[0] ^ k) * columns, columns), columns)]
        copies.append(pltpu.make_async_copy(block, to, sem.at[k]))
    for copy in copies:
        copy.start()
    for copy in copies:
        copy.wait()


def place(index, blocks):
    rows, columns = blocks[0].shape
    vmem = pl.BlockSpec(memory_space=pltpu.VMEM)
    return pl.pallas_call(
        place_kernel,
        out_shape=jax.ShapeDtypeStruct((rows, len(blocks) * columns), blocks[0].dtype),
        in_specs=[pl.BlockSpec(memory_space=pltpu.SMEM)] + [vmem] * len(blocks),
        out_specs=pl.BlockSpec(memory_space=pl.ANY),
        scratch_shapes=[pltpu.SemaphoreType.DMA((len(blocks),))],
        compiler_params=pltpu.CompilerParams(vmem_limit_bytes=8 * 1024 * 1024),
        name="place",
    )(index.reshape(1), *blocks)


def per_device(tokens, gate_weight, up_weight, down_weight, *, n_groups, n_batch, n_mp):
    n_row = n_batch // n_mp
    rows = tokens.shape[0]
    block, units = gate_weight.shape
    columns = down_weight.shape[1]
    axes = ("batch", "mp")
    batch = lax.axis_index("batch")
    core = lax.axis_index("mp")
    group = lax.axis_index("groups")
    row = batch // n_mp
    halved = n_groups == 2 and n_mp == 2 and n_row % 2 == 0
    near = n_row // 2 if halved else n_row

    def device(r, a, c):
        return (r * n_mp + a) * n_mp + c

    every = [(r, a, c) for r in range(n_row) for a in range(n_mp) for c in range(n_mp)]

    def swap(value, step):
        return lax.ppermute(
            value, axes, [(device(r, a, c), device(r ^ step, c, a)) for r, a, c in every]
        )

    def give_out(value, step):
        pairs = [
            (device(r, a, c), device(((r * n_mp + a) % n_row) ^ step, c, (r * n_mp + a) // n_row))
            for r, a, c in every
        ]
        return lax.ppermute(value, axes, pairs)

    def away(value, step):
        return lax.ppermute(value, "batch", [(b, b ^ step) for b in range(n_batch)])

    def others(value, axis, size):
        return [
            lax.ppermute(value, axis, [(c, c ^ step) for c in range(size)])
            for step in range(1, size)
        ]

    def cores(value):
        return in_order([value] + others(value, "mp", n_mp), core)

    def dot(left, right):
        return jnp.dot(left, right, preferred_element_type=jnp.float32)

    def halved_plan():
        size = rows // n_mp
        lane = batch % n_mp

        def weight_of(value):
            beside = away(value, 1)
            return [[value] + others(value, "mp", n_mp), [beside] + others(beside, "mp", n_mp)]

        gates, ups = weight_of(gate_weight), weight_of(up_weight)
        pieces = [piece for k in range(n_mp) for kind in (gates, ups) for piece in kind[k]]
        where = jnp.stack(
            [core * size]
            + [((row ^ s) * n_mp + (lane ^ k)) * block for s in range(n_row) for k in range(n_mp)]
        )
        slabs = list(cut(where, tokens, n_row, size, n_mp * block))
        for step in range(1, n_row):
            slabs[step] = away(slabs[step], step * n_mp)
        total, *sent = slab_sums(slabs, pieces, n_mp)
        for step in range(1, n_row):
            got = away(sent[step - 1], step * n_mp)
            total = total + got.astype(jnp.float32)
        gate = total[:, : n_mp * units]
        up = total[:, n_mp * units :]
        hidden = (jax.nn.silu(gate) * up).astype(jnp.bfloat16)
        hidden = jnp.concatenate(in_order([hidden[:, :units], hidden[:, units:]], core), axis=1)
        hidden = jnp.concatenate(cores(hidden), axis=0)

        side = row // near
        near_down = lax.ppermute(
            down_weight,
            axes,
            [(device(r, a, 1 - r // near), device(r, a, r // near)) for r in range(n_row) for a in range(2)],
        )
        far_down = lax.ppermute(
            down_weight,
            ("groups", "batch", "mp"),
            [
                (
                    g * n_batch * 2 + device(r, a, g),
                    g * n_batch * 2 + device(r ^ near, a, r // near),
                )
                for g in range(2)
                for r in range(n_row)
                for a in range(2)
            ],
        )
        holders = [device(r, a, 1 - r // near) for r in range(n_row) for a in range(2)]
        far_down_other = lax.ppermute(
            far_down,
            ("groups", "batch", "mp"),
            [(g * n_batch * 2 + h, (1 - g) * n_batch * 2 + h) for g in range(2) for h in holders],
        )
        own = core == side
        down = in_order(
            [jnp.where(own, down_weight, far_down), jnp.where(own, near_down, far_down_other)],
            jnp.where(own, core, group),
        )
        peers = range(1, near * n_mp)
        gathered = [hidden] + [away(hidden, k) for k in peers]
        result = dot(jnp.concatenate(gathered, axis=0), jnp.concatenate(down, axis=0))
        result = result.astype(jnp.bfloat16)
        blocks = [result[k * rows : (k + 1) * rows] for k in range(near * n_mp)]
        for k in peers:
            blocks[k] = away(blocks[k], k)
        return place(batch % (near * n_mp), blocks)

    if halved:
        return halved_plan()
    arrived = []
    for step in range(n_row):
        start = ((row ^ step) * n_mp + core) * block
        arrived.append(swap(lax.dynamic_slice_in_dim(tokens, start, block, 1), step))
    weights = cores(gate_weight) + cores(up_weight)
    weights = jnp.concatenate(weights, axis=1)
    down = jnp.concatenate(cores(down_weight), axis=0)
    total = 0.0
    for step in range(n_row):
        partial = dot(arrived[step], weights).astype(jnp.bfloat16)
        total = total + swap(partial, step).astype(jnp.float32)
    for part in others(total, "mp", n_mp):
        total = total + part
    gate = total[:, : n_mp * units]
    up = total[:, n_mp * units :]
    hidden = (jax.nn.silu(gate) * up).astype(jnp.bfloat16)
    stacked = jnp.stack([swap(hidden, step) for step in range(n_row)])
    mixed = jnp.zeros((rows, n_row * columns), jnp.bfloat16)
    for step in range(n_row):
        wanted = row ^ (batch % n_row) ^ step
        hidden_rows = lax.dynamic_index_in_dim(stacked, wanted, 0, keepdims=False)
        got = give_out(dot(hidden_rows, down).astype(jnp.bfloat16), step)
        mixed = lax.dynamic_update_slice_in_dim(mixed, got, (row ^ step) * columns, 1)
    return mixed


def solution(mesh):
    sizes = {f"n_{axis}": mesh.shape[axis] for axis in ("groups", "batch", "mp")}

    def body(*args):
        return per_device(*args, **sizes)

    return jax.shard_map(
        body,
        mesh=mesh,
        in_specs=(
            P(("groups", "batch"), None),
            P("batch", "mp"),
            P("batch", "mp"),
            P("mp", "batch"),
        ),
        out_specs=P(("groups", "batch"), "mp"),
        check_vma=False,
    )
```

```python
import functools

import jax
import jax.numpy as jnp
from jax import lax
from jax.experimental import pallas as pl
from jax.experimental.pallas import tpu as pltpu
from jax.sharding import PartitionSpec as P

N_FAR = 2


def in_order(parts, index):
    if len(parts) == 1:
        return parts
    if len(parts) == 2:
        first, second = parts
        return [jnp.where(index == 0, first, second), jnp.where(index == 0, second, first)]
    stack = jnp.take(jnp.stack(parts), index ^ jnp.arange(len(parts)), axis=0)
    return [stack[k] for k in range(len(parts))]


def cut_kernel(place, tokens, *refs, size):
    slabs, sem = refs[:-1], refs[-1]
    block = slabs[0].shape[1] // 2
    first_row = pl.multiple_of(place[0], size)
    copies = []
    for k in range(2 * len(slabs)):
        column = pl.multiple_of(place[1 + k], block)
        copies.append(
            pltpu.make_async_copy(
                tokens.at[pl.ds(first_row, size), pl.ds(column, block)],
                slabs[k // 2].at[:, pl.ds(k % 2 * block, block)],
                sem.at[k],
            )
        )
    for copy in copies:
        copy.start()
    for copy in copies:
        copy.wait()


def cut(place, tokens, n_slab, size, depth):
    slab = jax.ShapeDtypeStruct((size, depth), tokens.dtype)
    return pl.pallas_call(
        functools.partial(cut_kernel, size=size),
        out_shape=[slab] * n_slab,
        in_specs=[pl.BlockSpec(memory_space=pltpu.SMEM), pl.BlockSpec(memory_space=pltpu.HBM)],
        out_specs=[pl.BlockSpec(memory_space=pltpu.VMEM)] * n_slab,
        scratch_shapes=[pltpu.SemaphoreType.DMA((2 * n_slab,))],
        compiler_params=pltpu.CompilerParams(vmem_limit_bytes=8 * 1024 * 1024),
        name="cut",
    )(place, tokens)


def sums_kernel(*refs, n_slab, n_part):
    slabs, weights = refs[:n_slab], refs[n_slab : n_slab + 2 * n_part * n_part]
    outs = refs[n_slab + len(weights) : -1]
    slab_buf = refs[-1]
    size = slabs[0].shape[0]
    block, units = weights[0].shape
    for k, slab in enumerate(slabs):
        slab_buf[k * size : (k + 1) * size] = slab[...]
    wide = n_part * units
    for kind in range(2):
        total = None
        for part in range(n_part):
            first = (part * 2 + kind) * n_part
            product = jnp.dot(
                slab_buf[:, part * block : (part + 1) * block],
                jnp.concatenate([w[...] for w in weights[first : first + n_part]], axis=1),
                preferred_element_type=jnp.float32,
            )
            total = product if total is None else total + product
        for k, out in enumerate(outs):
            part_of = total[k * size : (k + 1) * size]
            out[:, kind * wide : (kind + 1) * wide] = part_of.astype(out.dtype)


def slab_sums(slabs, weights, n_part):
    n_slab = len(slabs)
    size, depth = slabs[0].shape
    wide = 2 * n_part * weights[0].shape[1]
    kept = jax.ShapeDtypeStruct((size, wide), jnp.float32)
    sent = jax.ShapeDtypeStruct((size, wide), jnp.bfloat16)
    vmem = pl.BlockSpec(memory_space=pltpu.VMEM)
    return pl.pallas_call(
        functools.partial(sums_kernel, n_slab=n_slab, n_part=n_part),
        out_shape=[kept] + [sent] * (n_slab - 1),
        in_specs=[vmem] * (n_slab + len(weights)),
        out_specs=[vmem] * n_slab,
        scratch_shapes=[pltpu.VMEM((n_slab * size, depth), jnp.bfloat16)],
        compiler_params=pltpu.CompilerParams(vmem_limit_bytes=16 * 1024 * 1024),
        name="slab_sums",
    )(*slabs, *weights)


def place_kernel(index, *refs):
    blocks, (out, sem) = refs[:-2], refs[-2:]
    columns = blocks[0].shape[1]
    copies = []
    for k, block in enumerate(blocks):
        to = out.at[:, pl.ds(pl.multiple_of((index[0] ^ k) * columns, columns), columns)]
        copies.append(pltpu.make_async_copy(block, to, sem.at[k]))
    for copy in copies:
        copy.start()
    for copy in copies:
        copy.wait()


def place(index, blocks):
    rows, columns = blocks[0].shape
    vmem = pl.BlockSpec(memory_space=pltpu.VMEM)
    return pl.pallas_call(
        place_kernel,
        out_shape=jax.ShapeDtypeStruct((rows, len(blocks) * columns), blocks[0].dtype),
        in_specs=[pl.BlockSpec(memory_space=pltpu.SMEM)] + [vmem] * len(blocks),
        out_specs=pl.BlockSpec(memory_space=pl.ANY),
        scratch_shapes=[pltpu.SemaphoreType.DMA((len(blocks),))],
        compiler_params=pltpu.CompilerParams(vmem_limit_bytes=8 * 1024 * 1024),
        name="place",
    )(index.reshape(1), *blocks)


def mixed_kernel(place, own_rows, beside_rows, *refs, n_hidden, n_far):
    hidden, far = refs[:n_hidden], refs[n_hidden : n_hidden + 2 * n_far]
    outs, down = refs[n_hidden + 2 * n_far : -1], refs[-1]
    rows = hidden[0].shape[0]
    units = own_rows.shape[0]
    own, core, group = place[0], place[1], place[2]

    @pl.when(own == 1)
    def _():
        down[pl.ds(pl.multiple_of(core * units, units), units)] = own_rows[...]
        down[pl.ds(pl.multiple_of((1 - core) * units, units), units)] = beside_rows[...]

    @pl.when(own != 1)
    def _():
        size = units // n_far
        for k, piece in enumerate(far):
            of = group if k < n_far else 1 - group
            first = pl.multiple_of(of * units + k % n_far * size, size)
            down[pl.ds(first, size)] = piece[...]

    result = jnp.dot(
        jnp.concatenate([h[...] for h in hidden], axis=0),
        down[...],
        preferred_element_type=jnp.float32,
    )
    for k, out in enumerate(outs):
        out[...] = result[k * rows : (k + 1) * rows].astype(out.dtype)


def mixed_blocks(place, own_rows, beside_rows, hidden, far):
    rows = hidden[0].shape[0]
    units, columns = own_rows.shape
    vmem = pl.BlockSpec(memory_space=pltpu.VMEM)
    return pl.pallas_call(
        functools.partial(mixed_kernel, n_hidden=len(hidden), n_far=len(far) // 2),
        out_shape=[jax.ShapeDtypeStruct((rows, columns), jnp.bfloat16)] * len(hidden),
        in_specs=[pl.BlockSpec(memory_space=pltpu.SMEM)] + [vmem] * (2 + len(hidden) + len(far)),
        out_specs=[vmem] * len(hidden),
        scratch_shapes=[pltpu.VMEM((2 * units, columns), jnp.bfloat16)],
        compiler_params=pltpu.CompilerParams(vmem_limit_bytes=16 * 1024 * 1024),
        name="mixed_blocks",
    )(place, own_rows, beside_rows, *hidden, *far)


def per_device(tokens, gate_weight, up_weight, down_weight, *, n_groups, n_batch, n_mp):
    n_row = n_batch // n_mp
    rows = tokens.shape[0]
    block, units = gate_weight.shape
    columns = down_weight.shape[1]
    axes = ("batch", "mp")
    batch = lax.axis_index("batch")
    core = lax.axis_index("mp")
    group = lax.axis_index("groups")
    row = batch // n_mp
    halved = n_groups == 2 and n_mp == 2 and n_row % 2 == 0
    near = n_row // 2 if halved else n_row

    def device(r, a, c):
        return (r * n_mp + a) * n_mp + c

    every = [(r, a, c) for r in range(n_row) for a in range(n_mp) for c in range(n_mp)]

    def swap(value, step):
        return lax.ppermute(
            value, axes, [(device(r, a, c), device(r ^ step, c, a)) for r, a, c in every]
        )

    def give_out(value, step):
        pairs = [
            (device(r, a, c), device(((r * n_mp + a) % n_row) ^ step, c, (r * n_mp + a) // n_row))
            for r, a, c in every
        ]
        return lax.ppermute(value, axes, pairs)

    def away(value, step):
        return lax.ppermute(value, "batch", [(b, b ^ step) for b in range(n_batch)])

    def others(value, axis, size):
        return [
            lax.ppermute(value, axis, [(c, c ^ step) for c in range(size)])
            for step in range(1, size)
        ]

    def cores(value):
        return in_order([value] + others(value, "mp", n_mp), core)

    def dot(left, right):
        return jnp.dot(left, right, preferred_element_type=jnp.float32)

    def halved_plan():
        size = rows // n_mp
        lane = batch % n_mp

        def weight_of(value):
            beside = away(value, 1)
            return [[value] + others(value, "mp", n_mp), [beside] + others(beside, "mp", n_mp)]

        gates, ups = weight_of(gate_weight), weight_of(up_weight)
        pieces = [piece for k in range(n_mp) for kind in (gates, ups) for piece in kind[k]]
        where = jnp.stack(
            [core * size]
            + [((row ^ s) * n_mp + (lane ^ k)) * block for s in range(n_row) for k in range(n_mp)]
        )
        slabs = list(cut(where, tokens, n_row, size, n_mp * block))
        for step in range(1, n_row):
            slabs[step] = away(slabs[step], step * n_mp)
        total, *sent = slab_sums(slabs, pieces, n_mp)
        for step in range(1, n_row):
            got = away(sent[step - 1], step * n_mp)
            total = total + got.astype(jnp.float32)
        gate = total[:, : n_mp * units]
        up = total[:, n_mp * units :]
        hidden = (jax.nn.silu(gate) * up).astype(jnp.bfloat16)
        hidden = jnp.concatenate(in_order([hidden[:, :units], hidden[:, units:]], core), axis=1)
        hidden = jnp.concatenate(cores(hidden), axis=0)

        side = row // near
        near_down = others(down_weight, "mp", n_mp)[0]
        wide = ("groups", "batch", "mp")
        fetch = []
        for g in range(2):
            for r in range(n_row):
                for a in range(2):
                    at = g * n_batch * 2
                    fetch.append((at + device(r, a, g), at + device(r ^ near, a, r // near)))
                    fetch.append((at + device(r, a, 1 - g), at + device(r, a, r // near)))
        holders = [device(r, a, 1 - r // near) for r in range(n_row) for a in range(2)]
        trade = [(g * n_batch * 2 + h, (1 - g) * n_batch * 2 + h) for g in range(2) for h in holders]
        far = []
        for part in range(N_FAR):
            size_of = units // N_FAR
            rows_of = down_weight[part * size_of : (part + 1) * size_of]
            far.append(lax.ppermute(rows_of, wide, fetch))
        for part in range(N_FAR):
            far.append(lax.ppermute(far[part], wide, trade))
        peers = range(1, near * n_mp)
        gathered = [hidden] + [away(hidden, k) for k in peers]
        flags = jnp.stack([(core == side).astype(jnp.int32), core, group])
        blocks = list(mixed_blocks(flags, down_weight, near_down, gathered, far))
        for k in peers:
            blocks[k] = away(blocks[k], k)
        return place(batch % (near * n_mp), blocks)

    if halved:
        return halved_plan()
    arrived = []
    for step in range(n_row):
        start = ((row ^ step) * n_mp + core) * block
        arrived.append(swap(lax.dynamic_slice_in_dim(tokens, start, block, 1), step))
    weights = cores(gate_weight) + cores(up_weight)
    weights = jnp.concatenate(weights, axis=1)
    down = jnp.concatenate(cores(down_weight), axis=0)
    total = 0.0
    for step in range(n_row):
        partial = dot(arrived[step], weights).astype(jnp.bfloat16)
        total = total + swap(partial, step).astype(jnp.float32)
    for part in others(total, "mp", n_mp):
        total = total + part
    gate = total[:, : n_mp * units]
    up = total[:, n_mp * units :]
    hidden = (jax.nn.silu(gate) * up).astype(jnp.bfloat16)
    stacked = jnp.stack([swap(hidden, step) for step in range(n_row)])
    mixed = jnp.zeros((rows, n_row * columns), jnp.bfloat16)
    for step in range(n_row):
        wanted = row ^ (batch % n_row) ^ step
        hidden_rows = lax.dynamic_index_in_dim(stacked, wanted, 0, keepdims=False)
        got = give_out(dot(hidden_rows, down).astype(jnp.bfloat16), step)
        mixed = lax.dynamic_update_slice_in_dim(mixed, got, (row ^ step) * columns, 1)
    return mixed


def solution(mesh):
    sizes = {f"n_{axis}": mesh.shape[axis] for axis in ("groups", "batch", "mp")}

    def body(*args):
        return per_device(*args, **sizes)

    return jax.shard_map(
        body,
        mesh=mesh,
        in_specs=(
            P(("groups", "batch"), None),
            P("batch", "mp"),
            P("batch", "mp"),
            P("mp", "batch"),
        ),
        out_specs=P(("groups", "batch"), "mp"),
        check_vma=False,
    )
```

```python
import functools

import jax
import jax.numpy as jnp
from jax import lax
from jax.experimental import pallas as pl
from jax.experimental.pallas import tpu as pltpu
from jax.sharding import PartitionSpec as P

N_FAR = 2


def in_order(parts, index):
    if len(parts) == 1:
        return parts
    if len(parts) == 2:
        first, second = parts
        return [jnp.where(index == 0, first, second), jnp.where(index == 0, second, first)]
    stack = jnp.take(jnp.stack(parts), index ^ jnp.arange(len(parts)), axis=0)
    return [stack[k] for k in range(len(parts))]


def cut_kernel(place, tokens, *refs, size):
    slabs, sem = refs[:-1], refs[-1]
    block = slabs[0].shape[1] // 2
    first_row = pl.multiple_of(place[0], size)
    copies = []
    for k in range(2 * len(slabs)):
        column = pl.multiple_of(place[1 + k], block)
        copies.append(
            pltpu.make_async_copy(
                tokens.at[pl.ds(first_row, size), pl.ds(column, block)],
                slabs[k // 2].at[:, pl.ds(k % 2 * block, block)],
                sem.at[k],
            )
        )
    for copy in copies:
        copy.start()
    for copy in copies:
        copy.wait()


def cut(place, tokens, n_slab, size, depth):
    slab = jax.ShapeDtypeStruct((size, depth), tokens.dtype)
    return pl.pallas_call(
        functools.partial(cut_kernel, size=size),
        out_shape=[slab] * n_slab,
        in_specs=[pl.BlockSpec(memory_space=pltpu.SMEM), pl.BlockSpec(memory_space=pltpu.HBM)],
        out_specs=[pl.BlockSpec(memory_space=pltpu.VMEM)] * n_slab,
        scratch_shapes=[pltpu.SemaphoreType.DMA((2 * n_slab,))],
        compiler_params=pltpu.CompilerParams(vmem_limit_bytes=8 * 1024 * 1024),
        name="cut",
    )(place, tokens)


def sums_kernel(*refs, n_slab, n_part):
    slabs, weights = refs[:n_slab], refs[n_slab : n_slab + 2 * n_part * n_part]
    outs = refs[n_slab + len(weights) : -1]
    slab_buf = refs[-1]
    size = slabs[0].shape[0]
    block, units = weights[0].shape
    for k, slab in enumerate(slabs):
        slab_buf[k * size : (k + 1) * size] = slab[...]
    wide = n_part * units
    for kind in range(2):
        total = None
        for part in range(n_part):
            first = (part * 2 + kind) * n_part
            product = jnp.dot(
                slab_buf[:, part * block : (part + 1) * block],
                jnp.concatenate([w[...] for w in weights[first : first + n_part]], axis=1),
                preferred_element_type=jnp.float32,
            )
            total = product if total is None else total + product
        for k, out in enumerate(outs):
            part_of = total[k * size : (k + 1) * size]
            out[:, kind * wide : (kind + 1) * wide] = part_of.astype(out.dtype)


def slab_sums(slabs, weights, n_part):
    n_slab = len(slabs)
    size, depth = slabs[0].shape
    wide = 2 * n_part * weights[0].shape[1]
    kept = jax.ShapeDtypeStruct((size, wide), jnp.float32)
    sent = jax.ShapeDtypeStruct((size, wide), jnp.bfloat16)
    vmem = pl.BlockSpec(memory_space=pltpu.VMEM)
    return pl.pallas_call(
        functools.partial(sums_kernel, n_slab=n_slab, n_part=n_part),
        out_shape=[kept] + [sent] * (n_slab - 1),
        in_specs=[vmem] * (n_slab + len(weights)),
        out_specs=[vmem] * n_slab,
        scratch_shapes=[pltpu.VMEM((n_slab * size, depth), jnp.bfloat16)],
        compiler_params=pltpu.CompilerParams(vmem_limit_bytes=16 * 1024 * 1024),
        name="slab_sums",
    )(*slabs, *weights)


def place_kernel(index, *refs):
    blocks, (out, sem) = refs[:-2], refs[-2:]
    columns = blocks[0].shape[1]
    copies = []
    for k, block in enumerate(blocks):
        to = out.at[:, pl.ds(pl.multiple_of((index[0] ^ k) * columns, columns), columns)]
        copies.append(pltpu.make_async_copy(block, to, sem.at[k]))
    for copy in copies:
        copy.start()
    for copy in copies:
        copy.wait()


def place(index, blocks):
    rows, columns = blocks[0].shape
    vmem = pl.BlockSpec(memory_space=pltpu.VMEM)
    return pl.pallas_call(
        place_kernel,
        out_shape=jax.ShapeDtypeStruct((rows, len(blocks) * columns), blocks[0].dtype),
        in_specs=[pl.BlockSpec(memory_space=pltpu.SMEM)] + [vmem] * len(blocks),
        out_specs=pl.BlockSpec(memory_space=pl.ANY),
        scratch_shapes=[pltpu.SemaphoreType.DMA((len(blocks),))],
        compiler_params=pltpu.CompilerParams(vmem_limit_bytes=8 * 1024 * 1024),
        name="place",
    )(index.reshape(1), *blocks)


def mixed_kernel(place, own_rows, beside_rows, *refs, n_hidden, n_far):
    hidden, far = refs[:n_hidden], refs[n_hidden : n_hidden + 2 * n_far]
    outs, down = refs[n_hidden + 2 * n_far : -1], refs[-1]
    rows = hidden[0].shape[0]
    units = own_rows.shape[0]
    own, core, group = place[0], place[1], place[2]

    @pl.when(own == 1)
    def _():
        down[pl.ds(pl.multiple_of(core * units, units), units)] = own_rows[...]
        down[pl.ds(pl.multiple_of((1 - core) * units, units), units)] = beside_rows[...]

    @pl.when(own != 1)
    def _():
        size = units // n_far
        for k, piece in enumerate(far):
            of = group if k < n_far else 1 - group
            first = pl.multiple_of(of * units + k % n_far * size, size)
            down[pl.ds(first, size)] = piece[...]

    result = jnp.dot(
        jnp.concatenate([h[...] for h in hidden], axis=0),
        down[...],
        preferred_element_type=jnp.float32,
    )
    for k, out in enumerate(outs):
        out[...] = result[k * rows : (k + 1) * rows].astype(out.dtype)


def mixed_blocks(place, own_rows, beside_rows, hidden, far):
    rows = hidden[0].shape[0]
    units, columns = own_rows.shape
    vmem = pl.BlockSpec(memory_space=pltpu.VMEM)
    return pl.pallas_call(
        functools.partial(mixed_kernel, n_hidden=len(hidden), n_far=len(far) // 2),
        out_shape=[jax.ShapeDtypeStruct((rows, columns), jnp.bfloat16)] * len(hidden),
        in_specs=[pl.BlockSpec(memory_space=pltpu.SMEM)] + [vmem] * (2 + len(hidden) + len(far)),
        out_specs=[vmem] * len(hidden),
        scratch_shapes=[pltpu.VMEM((2 * units, columns), jnp.bfloat16)],
        compiler_params=pltpu.CompilerParams(vmem_limit_bytes=16 * 1024 * 1024),
        name="mixed_blocks",
    )(place, own_rows, beside_rows, *hidden, *far)


def per_device(tokens, gate_weight, up_weight, down_weight, *, n_groups, n_batch, n_mp):
    n_row = n_batch // n_mp
    rows = tokens.shape[0]
    block, units = gate_weight.shape
    columns = down_weight.shape[1]
    axes = ("batch", "mp")
    batch = lax.axis_index("batch")
    core = lax.axis_index("mp")
    group = lax.axis_index("groups")
    row = batch // n_mp
    halved = n_groups == 2 and n_mp == 2 and n_row % 2 == 0
    near = n_row // 2 if halved else n_row

    def device(r, a, c):
        return (r * n_mp + a) * n_mp + c

    every = [(r, a, c) for r in range(n_row) for a in range(n_mp) for c in range(n_mp)]

    def swap(value, step):
        return lax.ppermute(
            value, axes, [(device(r, a, c), device(r ^ step, c, a)) for r, a, c in every]
        )

    def give_out(value, step):
        pairs = [
            (device(r, a, c), device(((r * n_mp + a) % n_row) ^ step, c, (r * n_mp + a) // n_row))
            for r, a, c in every
        ]
        return lax.ppermute(value, axes, pairs)

    def away(value, step):
        return lax.ppermute(value, "batch", [(b, b ^ step) for b in range(n_batch)])

    def others(value, axis, size):
        return [
            lax.ppermute(value, axis, [(c, c ^ step) for c in range(size)])
            for step in range(1, size)
        ]

    def cores(value):
        return in_order([value] + others(value, "mp", n_mp), core)

    def dot(left, right):
        return jnp.dot(left, right, preferred_element_type=jnp.float32)

    def halved_plan():
        size = rows // n_mp
        lane = batch % n_mp

        def weight_of(value):
            beside = away(value, 1)
            return [[value] + others(value, "mp", n_mp), [beside] + others(beside, "mp", n_mp)]

        gates, ups = weight_of(gate_weight), weight_of(up_weight)
        pieces = [piece for k in range(n_mp) for kind in (gates, ups) for piece in kind[k]]
        where = jnp.stack(
            [core * size]
            + [((row ^ s) * n_mp + (lane ^ k)) * block for s in range(n_row) for k in range(n_mp)]
        )
        slabs = list(cut(where, tokens, n_row, size, n_mp * block))
        for step in range(1, n_row):
            slabs[step] = away(slabs[step], step * n_mp)
        total, *sent = slab_sums(slabs, pieces, n_mp)
        for step in range(1, n_row):
            got = away(sent[step - 1], step * n_mp)
            total = total + got.astype(jnp.float32)
        gate = total[:, : n_mp * units]
        up = total[:, n_mp * units :]
        hidden = (jax.nn.silu(gate) * up).astype(jnp.bfloat16)
        hidden = jnp.concatenate(in_order([hidden[:, :units], hidden[:, units:]], core), axis=1)
        hidden = jnp.concatenate(cores(hidden), axis=0)

        side = row // near
        near_down = others(down_weight, "mp", n_mp)[0]
        wide = ("groups", "batch", "mp")
        fetch = []
        for g in range(2):
            for r in range(n_row):
                for a in range(2):
                    at = g * n_batch * 2
                    fetch.append((at + device(r, a, g), at + device(r ^ near, a, r // near)))
                    fetch.append((at + device(r, a, 1 - g), at + device(r, a, r // near)))
        holders = [device(r, a, 1 - r // near) for r in range(n_row) for a in range(2)]
        trade = [
            (g * n_batch * 2 + h, ((1 - g) if h in holders else g) * n_batch * 2 + h)
            for g in range(2)
            for h in range(n_batch * 2)
        ]
        far = []
        for part in range(N_FAR):
            size_of = units // N_FAR
            rows_of = down_weight[part * size_of : (part + 1) * size_of]
            far.append(lax.ppermute(rows_of, wide, fetch))
        for part in range(N_FAR):
            far.append(lax.ppermute(far[part], wide, trade))
        peers = range(1, near * n_mp)
        gathered = [hidden] + [away(hidden, k) for k in peers]
        flags = jnp.stack([(core == side).astype(jnp.int32), core, group])
        blocks = list(mixed_blocks(flags, down_weight, near_down, gathered, far))
        for k in peers:
            blocks[k] = away(blocks[k], k)
        return place(batch % (near * n_mp), blocks)

    if halved:
        return halved_plan()
    arrived = []
    for step in range(n_row):
        start = ((row ^ step) * n_mp + core) * block
        arrived.append(swap(lax.dynamic_slice_in_dim(tokens, start, block, 1), step))
    weights = cores(gate_weight) + cores(up_weight)
    weights = jnp.concatenate(weights, axis=1)
    down = jnp.concatenate(cores(down_weight), axis=0)
    total = 0.0
    for step in range(n_row):
        partial = dot(arrived[step], weights).astype(jnp.bfloat16)
        total = total + swap(partial, step).astype(jnp.float32)
    for part in others(total, "mp", n_mp):
        total = total + part
    gate = total[:, : n_mp * units]
    up = total[:, n_mp * units :]
    hidden = (jax.nn.silu(gate) * up).astype(jnp.bfloat16)
    stacked = jnp.stack([swap(hidden, step) for step in range(n_row)])
    mixed = jnp.zeros((rows, n_row * columns), jnp.bfloat16)
    for step in range(n_row):
        wanted = row ^ (batch % n_row) ^ step
        hidden_rows = lax.dynamic_index_in_dim(stacked, wanted, 0, keepdims=False)
        got = give_out(dot(hidden_rows, down).astype(jnp.bfloat16), step)
        mixed = lax.dynamic_update_slice_in_dim(mixed, got, (row ^ step) * columns, 1)
    return mixed


def solution(mesh):
    sizes = {f"n_{axis}": mesh.shape[axis] for axis in ("groups", "batch", "mp")}

    def body(*args):
        return per_device(*args, **sizes)

    return jax.shard_map(
        body,
        mesh=mesh,
        in_specs=(
            P(("groups", "batch"), None),
            P("batch", "mp"),
            P("batch", "mp"),
            P("mp", "batch"),
        ),
        out_specs=P(("groups", "batch"), "mp"),
        check_vma=False,
    )
```

```python
import functools

import jax
import jax.numpy as jnp
from jax import lax
from jax.experimental import pallas as pl
from jax.experimental.pallas import tpu as pltpu
from jax.sharding import PartitionSpec as P

N_FAR = 2


def in_order(parts, index):
    if len(parts) == 1:
        return parts
    if len(parts) == 2:
        first, second = parts
        return [jnp.where(index == 0, first, second), jnp.where(index == 0, second, first)]
    stack = jnp.take(jnp.stack(parts), index ^ jnp.arange(len(parts)), axis=0)
    return [stack[k] for k in range(len(parts))]


def cut_kernel(place, tokens, *refs, size):
    slabs, sem = refs[:-1], refs[-1]
    block = slabs[0].shape[1] // 2
    first_row = pl.multiple_of(place[0], size)
    copies = []
    for k in range(2 * len(slabs)):
        column = pl.multiple_of(place[1 + k], block)
        copies.append(
            pltpu.make_async_copy(
                tokens.at[pl.ds(first_row, size), pl.ds(column, block)],
                slabs[k // 2].at[:, pl.ds(k % 2 * block, block)],
                sem.at[k],
            )
        )
    for copy in copies:
        copy.start()
    for copy in copies:
        copy.wait()


def cut(place, tokens, n_slab, size, depth):
    slab = jax.ShapeDtypeStruct((size, depth), tokens.dtype)
    return pl.pallas_call(
        functools.partial(cut_kernel, size=size),
        out_shape=[slab] * n_slab,
        in_specs=[pl.BlockSpec(memory_space=pltpu.SMEM), pl.BlockSpec(memory_space=pltpu.HBM)],
        out_specs=[pl.BlockSpec(memory_space=pltpu.VMEM)] * n_slab,
        scratch_shapes=[pltpu.SemaphoreType.DMA((2 * n_slab,))],
        compiler_params=pltpu.CompilerParams(vmem_limit_bytes=8 * 1024 * 1024),
        name="cut",
    )(place, tokens)


def sums_kernel(*refs, n_slab, n_part):
    slabs, weights = refs[:n_slab], refs[n_slab : n_slab + 2 * n_part * n_part]
    outs = refs[n_slab + len(weights) : -1]
    slab_buf = refs[-1]
    size = slabs[0].shape[0]
    block, units = weights[0].shape
    for k, slab in enumerate(slabs):
        slab_buf[k * size : (k + 1) * size] = slab[...]
    wide = n_part * units
    for kind in range(2):
        total = None
        for part in range(n_part):
            first = (part * 2 + kind) * n_part
            product = jnp.dot(
                slab_buf[:, part * block : (part + 1) * block],
                jnp.concatenate([w[...] for w in weights[first : first + n_part]], axis=1),
                preferred_element_type=jnp.float32,
            )
            total = product if total is None else total + product
        for k, out in enumerate(outs):
            part_of = total[k * size : (k + 1) * size]
            out[:, kind * wide : (kind + 1) * wide] = part_of.astype(out.dtype)


def slab_sums(slabs, weights, n_part):
    n_slab = len(slabs)
    size, depth = slabs[0].shape
    wide = 2 * n_part * weights[0].shape[1]
    kept = jax.ShapeDtypeStruct((size, wide), jnp.float32)
    sent = jax.ShapeDtypeStruct((size, wide), jnp.bfloat16)
    vmem = pl.BlockSpec(memory_space=pltpu.VMEM)
    return pl.pallas_call(
        functools.partial(sums_kernel, n_slab=n_slab, n_part=n_part),
        out_shape=[kept] + [sent] * (n_slab - 1),
        in_specs=[vmem] * (n_slab + len(weights)),
        out_specs=[vmem] * n_slab,
        scratch_shapes=[pltpu.VMEM((n_slab * size, depth), jnp.bfloat16)],
        compiler_params=pltpu.CompilerParams(vmem_limit_bytes=16 * 1024 * 1024),
        name="slab_sums",
    )(*slabs, *weights)


def place_kernel(index, *refs):
    blocks, (out, sem) = refs[:-2], refs[-2:]
    columns = blocks[0].shape[1]
    copies = []
    for k, block in enumerate(blocks):
        to = out.at[:, pl.ds(pl.multiple_of((index[0] ^ k) * columns, columns), columns)]
        copies.append(pltpu.make_async_copy(block, to, sem.at[k]))
    for copy in copies:
        copy.start()
    for copy in copies:
        copy.wait()


def place(index, blocks):
    rows, columns = blocks[0].shape
    vmem = pl.BlockSpec(memory_space=pltpu.VMEM)
    return pl.pallas_call(
        place_kernel,
        out_shape=jax.ShapeDtypeStruct((rows, len(blocks) * columns), blocks[0].dtype),
        in_specs=[pl.BlockSpec(memory_space=pltpu.SMEM)] + [vmem] * len(blocks),
        out_specs=pl.BlockSpec(memory_space=pl.ANY),
        scratch_shapes=[pltpu.SemaphoreType.DMA((len(blocks),))],
        compiler_params=pltpu.CompilerParams(vmem_limit_bytes=8 * 1024 * 1024),
        name="place",
    )(index.reshape(1), *blocks)


def mixed_kernel(place, own_rows, beside_rows, *refs, n_hidden, n_far):
    hidden, far = refs[:n_hidden], refs[n_hidden : n_hidden + 2 * n_far]
    outs = refs[n_hidden + 2 * n_far :]
    rows = hidden[0].shape[0]
    units = own_rows.shape[0]
    own, core, group = place[0], place[1], place[2]

    stacked = jnp.concatenate([h[...] for h in hidden], axis=0)

    def give(index, first, second):
        low, high = stacked[:, :units], stacked[:, units:]
        result = jnp.dot(
            jnp.where(index == 0, low, high), first, preferred_element_type=jnp.float32
        ) + jnp.dot(jnp.where(index == 0, high, low), second, preferred_element_type=jnp.float32)
        for k, out in enumerate(outs):
            out[...] = result[k * rows : (k + 1) * rows].astype(out.dtype)

    @pl.when(own == 1)
    def _():
        give(core, own_rows[...], beside_rows[...])

    @pl.when(own != 1)
    def _():
        pieces = [piece[...] for piece in far]
        give(
            group,
            jnp.concatenate(pieces[:n_far], axis=0),
            jnp.concatenate(pieces[n_far:], axis=0),
        )


def mixed_blocks(place, own_rows, beside_rows, hidden, far):
    rows = hidden[0].shape[0]
    _, columns = own_rows.shape
    vmem = pl.BlockSpec(memory_space=pltpu.VMEM)
    return pl.pallas_call(
        functools.partial(mixed_kernel, n_hidden=len(hidden), n_far=len(far) // 2),
        out_shape=[jax.ShapeDtypeStruct((rows, columns), jnp.bfloat16)] * len(hidden),
        in_specs=[pl.BlockSpec(memory_space=pltpu.SMEM)] + [vmem] * (2 + len(hidden) + len(far)),
        out_specs=[vmem] * len(hidden),
        compiler_params=pltpu.CompilerParams(vmem_limit_bytes=16 * 1024 * 1024),
        name="mixed_blocks",
    )(place, own_rows, beside_rows, *hidden, *far)


def per_device(tokens, gate_weight, up_weight, down_weight, *, n_groups, n_batch, n_mp):
    n_row = n_batch // n_mp
    rows = tokens.shape[0]
    block, units = gate_weight.shape
    columns = down_weight.shape[1]
    axes = ("batch", "mp")
    batch = lax.axis_index("batch")
    core = lax.axis_index("mp")
    group = lax.axis_index("groups")
    row = batch // n_mp
    halved = n_groups == 2 and n_mp == 2 and n_row % 2 == 0
    near = n_row // 2 if halved else n_row

    def device(r, a, c):
        return (r * n_mp + a) * n_mp + c

    every = [(r, a, c) for r in range(n_row) for a in range(n_mp) for c in range(n_mp)]

    def swap(value, step):
        return lax.ppermute(
            value, axes, [(device(r, a, c), device(r ^ step, c, a)) for r, a, c in every]
        )

    def give_out(value, step):
        pairs = [
            (device(r, a, c), device(((r * n_mp + a) % n_row) ^ step, c, (r * n_mp + a) // n_row))
            for r, a, c in every
        ]
        return lax.ppermute(value, axes, pairs)

    def away(value, step):
        return lax.ppermute(value, "batch", [(b, b ^ step) for b in range(n_batch)])

    def others(value, axis, size):
        return [
            lax.ppermute(value, axis, [(c, c ^ step) for c in range(size)])
            for step in range(1, size)
        ]

    def cores(value):
        return in_order([value] + others(value, "mp", n_mp), core)

    def dot(left, right):
        return jnp.dot(left, right, preferred_element_type=jnp.float32)

    def halved_plan():
        size = rows // n_mp
        lane = batch % n_mp

        def weight_of(value):
            beside = away(value, 1)
            return [[value] + others(value, "mp", n_mp), [beside] + others(beside, "mp", n_mp)]

        gates, ups = weight_of(gate_weight), weight_of(up_weight)
        pieces = [piece for k in range(n_mp) for kind in (gates, ups) for piece in kind[k]]
        where = jnp.stack(
            [core * size]
            + [((row ^ s) * n_mp + (lane ^ k)) * block for s in range(n_row) for k in range(n_mp)]
        )
        slabs = list(cut(where, tokens, n_row, size, n_mp * block))
        for step in range(1, n_row):
            slabs[step] = away(slabs[step], step * n_mp)
        total, *sent = slab_sums(slabs, pieces, n_mp)
        for step in range(1, n_row):
            got = away(sent[step - 1], step * n_mp)
            total = total + got.astype(jnp.float32)
        gate = total[:, : n_mp * units]
        up = total[:, n_mp * units :]
        hidden = (jax.nn.silu(gate) * up).astype(jnp.bfloat16)
        hidden = jnp.concatenate(in_order([hidden[:, :units], hidden[:, units:]], core), axis=1)
        hidden = jnp.concatenate(cores(hidden), axis=0)

        side = row // near
        near_down = others(down_weight, "mp", n_mp)[0]
        wide = ("groups", "batch", "mp")
        fetch = []
        for g in range(2):
            for r in range(n_row):
                for a in range(2):
                    at = g * n_batch * 2
                    fetch.append((at + device(r, a, g), at + device(r ^ near, a, r // near)))
                    fetch.append((at + device(r, a, 1 - g), at + device(r, a, r // near)))
        holders = [device(r, a, 1 - r // near) for r in range(n_row) for a in range(2)]
        trade = [
            (g * n_batch * 2 + h, ((1 - g) if h in holders else g) * n_batch * 2 + h)
            for g in range(2)
            for h in range(n_batch * 2)
        ]
        far = []
        for part in range(N_FAR):
            size_of = units // N_FAR
            rows_of = down_weight[part * size_of : (part + 1) * size_of]
            far.append(lax.ppermute(rows_of, wide, fetch))
        for part in range(N_FAR):
            far.append(lax.ppermute(far[part], wide, trade))
        peers = range(1, near * n_mp)
        gathered = [hidden] + [away(hidden, k) for k in peers]
        flags = jnp.stack([(core == side).astype(jnp.int32), core, group])
        blocks = list(mixed_blocks(flags, down_weight, near_down, gathered, far))
        for k in peers:
            blocks[k] = away(blocks[k], k)
        return place(batch % (near * n_mp), blocks)

    if halved:
        return halved_plan()
    arrived = []
    for step in range(n_row):
        start = ((row ^ step) * n_mp + core) * block
        arrived.append(swap(lax.dynamic_slice_in_dim(tokens, start, block, 1), step))
    weights = cores(gate_weight) + cores(up_weight)
    weights = jnp.concatenate(weights, axis=1)
    down = jnp.concatenate(cores(down_weight), axis=0)
    total = 0.0
    for step in range(n_row):
        partial = dot(arrived[step], weights).astype(jnp.bfloat16)
        total = total + swap(partial, step).astype(jnp.float32)
    for part in others(total, "mp", n_mp):
        total = total + part
    gate = total[:, : n_mp * units]
    up = total[:, n_mp * units :]
    hidden = (jax.nn.silu(gate) * up).astype(jnp.bfloat16)
    stacked = jnp.stack([swap(hidden, step) for step in range(n_row)])
    mixed = jnp.zeros((rows, n_row * columns), jnp.bfloat16)
    for step in range(n_row):
        wanted = row ^ (batch % n_row) ^ step
        hidden_rows = lax.dynamic_index_in_dim(stacked, wanted, 0, keepdims=False)
        got = give_out(dot(hidden_rows, down).astype(jnp.bfloat16), step)
        mixed = lax.dynamic_update_slice_in_dim(mixed, got, (row ^ step) * columns, 1)
    return mixed


def solution(mesh):
    sizes = {f"n_{axis}": mesh.shape[axis] for axis in ("groups", "batch", "mp")}

    def body(*args):
        return per_device(*args, **sizes)

    return jax.shard_map(
        body,
        mesh=mesh,
        in_specs=(
            P(("groups", "batch"), None),
            P("batch", "mp"),
            P("batch", "mp"),
            P("mp", "batch"),
        ),
        out_specs=P(("groups", "batch"), "mp"),
        check_vma=False,
    )
```
